32 devices in a mesh: dp: 8 (over z, y), tensor: 4 (over x, core).
Axes of the slice: x: 2, y: 2, z: 4, core: 2. Of those that a mesh axis runs over, the one named last changes fastest.
Arguments:
- layer_in: bfloat16 [4096, 768], P(('dp', 'tensor')), may hold values from -6 to 6
- encoder_states: bfloat16 [4096, 768], P(('dp', 'tensor')), may hold values from -6 to 6
- grad_out: bfloat16 [4096, 768], P(('dp', 'tensor')), may hold values from -6 to 6
- buckets: int32 [8, 512, 512], P('dp'), may hold values from 0 to 31, as said below
- keep: int32 [8, 512, 512], P('dp'), may hold values from 0 to 1, as said below
- wq_self: bfloat16 [768, 768], P('dp', 'tensor'), may hold values from -0.02734375 to 0.02734375
- wk_self: bfloat16 [768, 768], P('dp', 'tensor'), may hold values from -0.21875 to 0.21875
- wv_self: bfloat16 [768, 768], P('dp', 'tensor'), may hold values from -0.21875 to 0.21875
- wo_self: bfloat16 [768, 768], P('tensor', 'dp'), may hold values from -0.875 to 0.875
- wq_cross: bfloat16 [768, 768], P('dp', 'tensor'), may hold values from -0.02734375 to 0.02734375
- wk_cross: bfloat16 [768, 768], P('dp', 'tensor'), may hold values from -0.21875 to 0.21875
- wv_cross: bfloat16 [768, 768], P('dp', 'tensor'), may hold values from -0.21875 to 0.21875
- wo_cross: bfloat16 [768, 768], P('tensor', 'dp'), may hold values from -0.875 to 0.875
- w_gate: bfloat16 [768, 2048], P('dp', 'tensor'), may hold values from -0.21875 to 0.21875
- w_up: bfloat16 [768, 2048], P('dp', 'tensor'), may hold values from -0.21875 to 0.21875
- w_down: bfloat16 [2048, 768], P('tensor', 'dp'), may hold values from -0.125 to 0.125
- norm_scales: bfloat16 [3, 768], P(None, 'dp'), may hold values from 0.5 to 1.5
- rel_bias: float32 [32, 12], P(None, 'tensor'), may hold values from -4 to 4
Outputs:
- layer_out: bfloat16 [4096, 768], P(('dp', 'tensor'))
- grad_in: float32 [4096, 768], P(('dp', 'tensor'))
- grad_encoder: float32 [4096, 768], P(('dp', 'tensor'))
- grad_wq_self: float32 [768, 768], P('dp', 'tensor')
- grad_wk_self: float32 [768, 768], P('dp', 'tensor')
- grad_wv_self: float32 [768, 768], P('dp', 'tensor')
- grad_wo_self: float32 [768, 768], P('tensor', 'dp')
- grad_wq_cross: float32 [768, 768], P('dp', 'tensor')
- grad_wk_cross: float32 [768, 768], P('dp', 'tensor')
- grad_wv_cross: float32 [768, 768], P('dp', 'tensor')
- grad_wo_cross: float32 [768, 768], P('tensor', 'dp')
- grad_w_gate: float32 [768, 2048], P('dp', 'tensor')
- grad_w_up: float32 [768, 2048], P('dp', 'tensor')
- grad_w_down: float32 [2048, 768], P('tensor', 'dp')
- grad_norm_scales: float32 [3, 768], P(None, ('dp', 'tensor'))
- grad_rel_bias: float32 [32, 12], P(None, 'tensor')
The draws below stay inside these ranges and needn't reach their ends.
Inputs may be any that keep to these rules, and one draw needn't show every extreme that they name: Each sequence holds one to three documents, the first of 256 positions or more. buckets[s, i, j] is the T5 bucket (exact below 16, logarithmic up to distance 128, the last bucket beyond) of i - j where keep = 1, and 0 elsewhere. keep[s, i, j] = 1 exactly where key j lies in the same document as query i and j <= i.
All inputs are finite; a program needn't handle non-finite values.
Results may differ from the reference program's by a relative error of at most 0.02.
Values may be sent and summed in bfloat16 or wider, within the bound.
A program may use at most 128 MiB of HBM per device.

```python
import math
import jax
import jax.numpy as jnp
import numpy as np
from jax import lax

D = 768
H = 12
DH = 64
FF = 2048
NBUCKET = 32
L = 512
HD = 768
SEQS = 8
TOKENS = 4096


def distance_table(length):
    exact_count = NBUCKET // 2
    bucket_table = np.zeros(length, dtype=np.int32)
    for distance in range(length):
        if distance < exact_count:
            bucket_table[distance] = distance
        else:
            spread = int(math.log(distance / exact_count) / math.log(128 / exact_count) * (NBUCKET - exact_count))
            bucket_table[distance] = min(exact_count + spread, NBUCKET - 1)
    return bucket_table


def doc_layout(key):
    base_key = jax.random.fold_in(key, 11)
    bucket_table = jnp.asarray(distance_table(L))

    def sequence_layout(number):
        cuts = jax.random.randint(jax.random.fold_in(base_key, number), (2,), L // 2, L + L // 4)
        places = lax.iota(jnp.int32, L)
        documents = (places >= cuts[0]).astype(jnp.int32) + (places >= cuts[1]).astype(jnp.int32)
        distance = places[:, None] - places[None, :]
        allowed = (documents[:, None] == documents[None, :]) & (distance >= 0)
        bucket_rows = jnp.where(allowed, bucket_table[jnp.clip(distance, 0, L - 1)], 0)
        return (bucket_rows.astype(jnp.int32), allowed.astype(jnp.int32))
    return lax.map(sequence_layout, lax.iota(jnp.int32, SEQS))


def draw_buckets(key, part):
    return doc_layout(key)[0]


def draw_keep(key, part):
    return doc_layout(key)[1]


def block_scale(key, dims, split, smallest, largest):
    loudness = 1.0
    for axis_at, shards_of in split:
        steps = jax.random.uniform(jax.random.fold_in(jax.random.fold_in(key, 6), axis_at), (shards_of,), jnp.float32, smallest / len(split), largest / len(split))
        loudness = loudness * jnp.repeat(jnp.exp(steps), dims[axis_at] // shards_of).reshape((-1,) + (1,) * (len(dims) - 1 - axis_at))
    return loudness


def centred(stream_key, extent, scale, reach, cuts=(), kind=jnp.bfloat16):
    entries = scale * jax.random.normal(stream_key, extent, jnp.float32)
    if cuts:
        entries = entries * block_scale(stream_key, extent, cuts, -0.22, 0.18)
    return jnp.clip(entries, -reach, reach).astype(kind)


def setup_inputs(seed: int = 0) -> dict:
    key_list = jax.random.split(jax.random.key(seed), 19)
    return {
        "layer_in": centred(key_list[0], (TOKENS, D), 1.0, 6.0, ((0, 32),)),
        "encoder_states": centred(key_list[1], (TOKENS, D), 1.0, 6.0, ((0, 32),)),
        "grad_out": centred(key_list[2], (TOKENS, D), 1.0, 6.0, ((0, 32),)),
        "buckets": draw_buckets(jax.random.fold_in(key_list[18], 71), 0),
        "keep": draw_keep(jax.random.fold_in(key_list[18], 71), 0),
        "wq_self": centred(key_list[5], (D, HD), (D * DH) ** -0.5, 0.02734375, ((0, 8), (1, 4))),
        "wk_self": centred(key_list[6], (D, HD), D ** -0.5, 0.21875, ((0, 8), (1, 4))),
        "wv_self": centred(key_list[7], (D, HD), D ** -0.5, 0.21875, ((0, 8), (1, 4))),
        "wo_self": centred(key_list[8], (HD, D), (HD // 16) ** -0.5, 0.875, ((0, 4), (1, 8))),
        "wq_cross": centred(key_list[9], (D, HD), (D * DH) ** -0.5, 0.02734375, ((0, 8), (1, 4))),
        "wk_cross": centred(key_list[10], (D, HD), D ** -0.5, 0.21875, ((0, 8), (1, 4))),
        "wv_cross": centred(key_list[11], (D, HD), D ** -0.5, 0.21875, ((0, 8), (1, 4))),
        "wo_cross": centred(key_list[12], (HD, D), (HD // 16) ** -0.5, 0.875, ((0, 4), (1, 8))),
        "w_gate": centred(key_list[13], (D, FF), D ** -0.5, 0.21875, ((0, 8), (1, 4))),
        "w_up": centred(key_list[14], (D, FF), D ** -0.5, 0.21875, ((0, 8), (1, 4))),
        "w_down": centred(key_list[15], (FF, D), FF ** -0.5, 0.125, ((0, 4), (1, 8))),
        "norm_scales": jnp.clip(1.0 + 0.1 * jax.random.normal(key_list[16], (3, D), jnp.float32), 0.5, 1.5).astype(jnp.bfloat16),
        "rel_bias": centred(key_list[17], (NBUCKET, H), 0.8, 4.0, ((1, 4),), jnp.float32),
    }


NORM_EPSILON = 1e-06
MASKED_SCORE = -1e+30
GELU_CUBIC = 0.044715

def to_half(values):
    return values.astype(jnp.bfloat16)

def matmul(left_side, right_side):
    return jnp.dot(left_side, right_side, preferred_element_type=jnp.float32)

def left_contract(left_side, right_side):
    return jnp.dot(left_side.T, right_side, preferred_element_type=jnp.float32)

def right_contract(left_side, right_side):
    return jnp.dot(left_side, right_side.T, preferred_element_type=jnp.float32)

def gelu_pair(values):
    root_scale = math.sqrt(2.0 / math.pi)
    interior = root_scale * (values + GELU_CUBIC * values * values * values)
    tangent = jnp.tanh(interior)
    activated = 0.5 * values * (1.0 + tangent)
    slope = 0.5 * (1.0 + tangent) + 0.5 * values * (1.0 - tangent * tangent) * root_scale * (1.0 + 3.0 * GELU_CUBIC * values * values)
    return (activated, slope)

def norm_forward(stream, gain):
    inverse = lax.rsqrt(lax.optimization_barrier(jnp.mean(stream * stream, axis=-1, keepdims=True)) + NORM_EPSILON)
    unit_rows = stream * inverse
    return (unit_rows, inverse, to_half(unit_rows * gain.astype(jnp.float32)))

def norm_backward(incoming, unit_rows, inverse, gain):
    scaled = incoming * gain.astype(jnp.float32)
    result = inverse * (scaled - unit_rows * lax.optimization_barrier(jnp.mean(scaled * unit_rows, axis=-1, keepdims=True)))
    return (result, lax.optimization_barrier(jnp.sum(incoming * unit_rows, axis=0)))

def head_split(matrix):
    return matrix.reshape(matrix.shape[0], -1, DH).astype(jnp.float32)

def score_matrix(queries, keys, bias, allowed):
    logits = jnp.einsum('qhd,khd->hqk', head_split(queries), head_split(keys))
    if bias is not None:
        logits = jnp.where(allowed[None], logits + bias, MASKED_SCORE)
    return logits

def attend(queries, keys, values, bias, allowed):
    logits = score_matrix(queries, keys, bias, allowed)
    row_max = lax.optimization_barrier(jnp.max(logits, axis=-1, keepdims=True))
    log_total = row_max + jnp.log(lax.optimization_barrier(jnp.sum(jnp.exp(logits - row_max), axis=-1, keepdims=True)))
    probs_half = lax.optimization_barrier(to_half(jnp.exp(logits - log_total))).astype(jnp.float32)
    mixed = jnp.einsum('hqk,khd->qhd', probs_half, head_split(values))
    return (to_half(mixed.reshape(queries.shape[0], -1)), log_total)

def attend_back(queries, keys, values, bias, allowed, log_total, grad_mixed):
    logits = score_matrix(queries, keys, bias, allowed)
    probs_full = jnp.exp(logits - log_total)
    probs_half = lax.optimization_barrier(to_half(probs_full)).astype(jnp.float32)
    grad_values = to_half(jnp.einsum('hqk,qhd->khd', probs_half, head_split(grad_mixed)).reshape(keys.shape[0], -1))
    grad_probs = jnp.einsum('qhd,khd->hqk', head_split(grad_mixed), head_split(values))
    centre = lax.optimization_barrier(jnp.sum(probs_full * grad_probs, axis=-1, keepdims=True))
    grad_logits = probs_full * (grad_probs - centre)
    logits_half = lax.optimization_barrier(to_half(grad_logits)).astype(jnp.float32)
    grad_queries = to_half(jnp.einsum('hqk,khd->qhd', logits_half, head_split(keys)).reshape(queries.shape[0], -1))
    grad_keys = to_half(jnp.einsum('hqk,qhd->khd', logits_half, head_split(queries)).reshape(keys.shape[0], -1))
    return (grad_queries, grad_keys, grad_values, grad_logits)

def one_sequence(stream_rows, source_rows, grad_rows, bucket_rows, keep_rows, params):
    wq_self, wk_self, wv_self, wo_self, wq_cross, wk_cross, wv_cross, wo_cross, w_gate, w_up, w_down, norm_scales, rel_bias = params
    allowed = keep_rows == 1
    bias_self = jnp.transpose(rel_bias[bucket_rows], (2, 0, 1))
    stream_in = stream_rows.astype(jnp.float32)
    unit_one, inverse_one, first_normed_input = norm_forward(stream_in, norm_scales[0])
    self_q = to_half(matmul(first_normed_input, wq_self))
    self_k = to_half(matmul(first_normed_input, wk_self))
    self_v = to_half(matmul(first_normed_input, wv_self))
    mixed_self, total_self = attend(self_q, self_k, self_v, bias_self, allowed)
    stream_one = stream_in + matmul(mixed_self, wo_self)
    unit_two, inverse_two, normed_two = norm_forward(stream_one, norm_scales[1])
    cross_q = to_half(matmul(normed_two, wq_cross))
    cross_k = to_half(matmul(source_rows, wk_cross))
    cross_v = to_half(matmul(source_rows, wv_cross))
    mixed_cross, total_cross = attend(cross_q, cross_k, cross_v, None, None)
    stream_two = stream_one + matmul(mixed_cross, wo_cross)
    unit_three, inverse_three, normed_three = norm_forward(stream_two, norm_scales[2])
    gate_rows = matmul(normed_three, w_gate)
    up_rows = matmul(normed_three, w_up)
    activated, slope = gelu_pair(gate_rows)
    hidden = to_half(activated * up_rows)
    layer_rows = to_half(stream_two + matmul(hidden, w_down))
    grad_hidden = right_contract(grad_rows, w_down)
    grad_w_down = left_contract(hidden, grad_rows)
    grad_gate = to_half(grad_hidden * up_rows * slope)
    grad_up = to_half(grad_hidden * activated)
    grad_w_gate = left_contract(normed_three, grad_gate)
    grad_w_up = left_contract(normed_three, grad_up)
    grad_normed_three = right_contract(grad_gate, w_gate) + right_contract(grad_up, w_up)
    back_three, gain_three = norm_backward(grad_normed_three, unit_three, inverse_three, norm_scales[2])
    grad_stream_two = grad_rows.astype(jnp.float32) + back_three
    grad_two_half = to_half(grad_stream_two)
    grad_mixed_cross = to_half(right_contract(grad_two_half, wo_cross))
    grad_wo_cross = left_contract(mixed_cross, grad_two_half)
    grad_q_cross, cross_key_gradient, grad_v_cross, unused_logits = attend_back(cross_q, cross_k, cross_v, None, None, total_cross, grad_mixed_cross)
    grad_wq_cross = left_contract(normed_two, grad_q_cross)
    grad_wk_cross = left_contract(source_rows, cross_key_gradient)
    grad_wv_cross = left_contract(source_rows, grad_v_cross)
    grad_source = right_contract(cross_key_gradient, wk_cross) + right_contract(grad_v_cross, wv_cross)
    back_two, gain_two = norm_backward(right_contract(grad_q_cross, wq_cross), unit_two, inverse_two, norm_scales[1])
    grad_stream_one = grad_stream_two + back_two
    grad_one_half = to_half(grad_stream_one)
    grad_mixed_self = to_half(right_contract(grad_one_half, wo_self))
    grad_wo_self = left_contract(mixed_self, grad_one_half)
    grad_q_self, grad_k_self, grad_v_self, grad_logits_self = attend_back(self_q, self_k, self_v, bias_self, allowed, total_self, grad_mixed_self)
    grad_bias = jax.ops.segment_sum(jnp.transpose(grad_logits_self, (1, 2, 0)).reshape(-1, grad_logits_self.shape[0]), bucket_rows.reshape(-1), num_segments=NBUCKET)
    grad_wq_self = left_contract(first_normed_input, grad_q_self)
    grad_wk_self = left_contract(first_normed_input, grad_k_self)
    grad_wv_self = left_contract(first_normed_input, grad_v_self)
    grad_normed_one = right_contract(grad_q_self, wq_self) + right_contract(grad_k_self, wk_self) + right_contract(grad_v_self, wv_self)
    back_one, gain_one = norm_backward(grad_normed_one, unit_one, inverse_one, norm_scales[0])
    grad_stream_in = grad_stream_one + back_one
    grads = (grad_wq_self, grad_wk_self, grad_wv_self, grad_wo_self, grad_wq_cross, grad_wk_cross, grad_wv_cross, grad_wo_cross, grad_w_gate, grad_w_up, grad_w_down, jnp.stack([gain_one, gain_two, gain_three]), grad_bias)
    return (layer_rows, grad_stream_in, grad_source, grads)

def add_pair(first, second):
    return first + second

def reference(layer_in, encoder_states, grad_out, buckets, keep, wq_self, wk_self, wv_self, wo_self, wq_cross, wk_cross, wv_cross, wo_cross, w_gate, w_up, w_down, norm_scales, rel_bias):
    params = (wq_self, wk_self, wv_self, wo_self, wq_cross, wk_cross, wv_cross, wo_cross, w_gate, w_up, w_down, norm_scales, rel_bias)
    zero_grads = tuple((jnp.zeros(param.shape, jnp.float32) for param in params))

    def step(summed_totals, pieces):
        layer_rows, grad_stream_in, grad_source, grads = one_sequence(pieces[0], pieces[1], pieces[2], pieces[3], pieces[4], params)
        return (jax.tree.map(add_pair, summed_totals, grads), (layer_rows, grad_stream_in, grad_source))
    sequences = (layer_in.reshape(SEQS, L, D), encoder_states.reshape(SEQS, L, D), grad_out.reshape(SEQS, L, D), buckets, keep)
    summed_totals, outputs = lax.scan(step, zero_grads, sequences)
    return (outputs[0].reshape(TOKENS, D), outputs[1].reshape(TOKENS, D), outputs[2].reshape(TOKENS, D), summed_totals[0], summed_totals[1], summed_totals[2], summed_totals[3], summed_totals[4], summed_totals[5], summed_totals[6], summed_totals[7], summed_totals[8], summed_totals[9], summed_totals[10], summed_totals[11], summed_totals[12])
```

```python
import math

import jax
import jax.numpy as jnp
import numpy as np
from jax import lax
from jax.experimental import pallas as pl
from jax.experimental.pallas import tpu as pltpu
from jax.sharding import PartitionSpec as P

DH = 64
NBUCKET = 32
L = 512
BLOCK = 128
NORM_EPSILON = 1e-06
MASKED_SCORE = -1e30
GELU_CUBIC = 0.044715
F32 = jnp.float32
BF16 = jnp.bfloat16


def to_half(values):
    return values.astype(BF16)


def matmul(left_side, right_side):
    return jnp.dot(left_side, right_side, preferred_element_type=F32)


def left_contract(left_side, right_side):
    return lax.dot_general(left_side, right_side, (((0,), (0,)), ((), ())), preferred_element_type=F32)


def right_contract(left_side, right_side):
    return lax.dot_general(left_side, right_side, (((1,), (1,)), ((), ())), preferred_element_type=F32)


def gelu_pair(values):
    root_scale = math.sqrt(2.0 / math.pi)
    interior = root_scale * (values + GELU_CUBIC * values * values * values)
    tangent = jnp.tanh(interior)
    activated = 0.5 * values * (1.0 + tangent)
    slope = 0.5 * (1.0 + tangent) + 0.5 * values * (1.0 - tangent * tangent) * root_scale * (
        1.0 + 3.0 * GELU_CUBIC * values * values
    )
    return (activated, slope)


def unit_norm(stream):
    inverse = lax.rsqrt(jnp.mean(stream * stream, axis=-1, keepdims=True) + NORM_EPSILON)
    return (stream * inverse, inverse)


def norm_backward(incoming, unit_rows, inverse, gain):
    scaled = incoming * gain
    result = inverse * (scaled - unit_rows * jnp.mean(scaled * unit_rows, axis=-1, keepdims=True))
    return (result, jnp.sum(incoming * unit_rows, axis=0))


def spread(rows_local):
    return lax.all_gather(rows_local, "tensor", axis=0, tiled=True)


def collect(partial_rows):
    return lax.psum_scatter(to_half(partial_rows), "tensor", scatter_dimension=0, tiled=True).astype(F32)


def distance_indicator():
    exact = NBUCKET // 2
    distance = (-np.arange(L)) % L
    log_part = exact + np.floor(
        np.log(np.maximum(distance, 1) / exact) / np.log(128 / exact) * (NBUCKET - exact)
    ).astype(np.int64)
    bucket = np.where(distance < exact, distance, np.minimum(log_part, NBUCKET - 1))
    return (bucket[None, :] == np.arange(NBUCKET)[:, None]).astype(np.float32)


def whole(*shape_and_type):
    return jax.ShapeDtypeStruct(*shape_and_type)


def call(kernel, outs, scratch=(), name=None):
    return pl.pallas_call(
        kernel,
        out_shape=outs,
        scratch_shapes=list(scratch),
        name=name,
        compiler_params=pltpu.CompilerParams(vmem_limit_bytes=60 * 1024 * 1024),
    )


def attend_block(q, k, v, bias, allowed):
    logits = right_contract(q, k)
    if bias is not None:
        logits = jnp.where(allowed, logits + bias, MASKED_SCORE)
    row_max = jnp.max(logits, axis=-1, keepdims=True)
    powers = jnp.exp(logits - row_max)
    probs = to_half(powers / jnp.sum(powers, axis=-1, keepdims=True))
    return probs, to_half(matmul(probs, v))


def attend_kernel(masked, qkv_ref, *refs):
    if masked:
        base_ref, keep_ref, mixed_ref, probs_ref = refs
    else:
        mixed_ref, probs_ref = refs
    width = mixed_ref.shape[1]
    heads = width // DH
    for block in range(L // BLOCK):
        rows = slice(block * BLOCK, (block + 1) * BLOCK)
        reach = (block + 1) * BLOCK if masked else L
        allowed = keep_ref[rows, :reach] == 1 if masked else None
        pieces = []
        for h in range(heads):
            bias = None
            if masked:
                base = base_ref[h]
                tiles = [
                    pltpu.roll(base, 8 * t, 1) if t else base
                    for t in range(block * BLOCK // 8, (block + 1) * BLOCK // 8)
                ]
                bias = jnp.concatenate(tiles, axis=0)[:, :reach]
            probs, mixed = attend_block(
                qkv_ref[rows, h * DH:(h + 1) * DH],
                qkv_ref[:reach, width + h * DH:width + (h + 1) * DH],
                qkv_ref[:reach, 2 * width + h * DH:2 * width + (h + 1) * DH],
                bias,
                allowed,
            )
            probs_ref[h, rows, :reach] = probs
            pieces.append(mixed)
        mixed_ref[rows, :] = jnp.concatenate(pieces, axis=1)


def attend_back_kernel(masked, qkv_ref, probs_ref, gm_ref, grad_ref, *refs):
    if masked:
        diag_ref, key_total, value_total = refs
    else:
        key_total, value_total = refs
    width = gm_ref.shape[1]
    heads = width // DH
    for h in range(heads):
        cq = slice(h * DH, (h + 1) * DH)
        ck = slice(width + h * DH, width + (h + 1) * DH)
        cv = slice(2 * width + h * DH, 2 * width + (h + 1) * DH)
        diag = jnp.zeros((8, L), F32)
        for block in reversed(range(L // BLOCK)):
            rows = slice(block * BLOCK, (block + 1) * BLOCK)
            reach = (block + 1) * BLOCK if masked else L
            probs = probs_ref[h, rows, :reach]
            gm = gm_ref[rows, cq]
            grad_probs = right_contract(gm, qkv_ref[:reach, cv])
            probs_full = probs.astype(F32)
            centre = jnp.sum(probs_full * grad_probs, axis=-1, keepdims=True)
            grad_logits = probs_full * (grad_probs - centre)
            half = to_half(grad_logits)
            grad_ref[rows, cq] = to_half(matmul(half, qkv_ref[:reach, ck]))
            key_part = left_contract(half, qkv_ref[rows, cq])
            value_part = left_contract(probs, gm)
            if block == L // BLOCK - 1:
                key_total[:, :] = key_part
                value_total[:, :] = value_part
            else:
                key_total[:reach, :] += key_part
                value_total[:reach, :] += value_part
            if masked:
                for t in range(BLOCK // 8):
                    tile = grad_logits[8 * t:8 * t + 8]
                    if reach < L:
                        tile = jnp.concatenate([tile, jnp.zeros((8, L - reach), F32)], axis=1)
                    shift = (L - (block * BLOCK + 8 * t)) % L
                    diag = diag + (pltpu.roll(tile, shift, 1) if shift else tile)
        grad_ref[:, ck] = to_half(key_total[...])
        grad_ref[:, cv] = to_half(value_total[...])
        if masked:
            total = diag[0:1]
            for s in range(1, 8):
                total = total + pltpu.roll(diag[s:s + 1], L - s, 1)
            diag_ref[h:h + 1, :] = total


def attend(qkv, base, keep):
    width = qkv.shape[1] // 3
    outs = (
        whole((L, width), BF16),
        whole((width // DH, L, L), BF16),
    )
    if base is None:
        return call(lambda *r: attend_kernel(False, *r), outs, name="cross_fwd")(qkv)
    return call(lambda *r: attend_kernel(True, *r), outs, name="self_fwd")(qkv, base, keep)


def attend_back(qkv, probs, grad_mixed, masked):
    width = qkv.shape[1] // 3
    scratch = (pltpu.VMEM((L, DH), F32), pltpu.VMEM((L, DH), F32))
    grads = whole((L, 3 * width), BF16)
    if masked:
        return call(
            lambda *r: attend_back_kernel(True, *r),
            (grads, whole((width // DH, L), F32)),
            scratch,
            name="self_bwd",
        )(qkv, probs, grad_mixed)
    return call(lambda *r: attend_back_kernel(False, *r), grads, scratch, name="cross_bwd")(
        qkv, probs, grad_mixed
    )


def gather_weights(*parts):
    return lax.all_gather(jnp.concatenate(parts, axis=1), "dp", axis=0, tiled=True)


def scatter_grads(*parts):
    return lax.psum_scatter(to_half(jnp.concatenate(parts, axis=1)), "dp", scatter_dimension=0, tiled=True).astype(F32)


def per_device(
    layer_in,
    encoder_states,
    grad_out,
    buckets,
    keep,
    wq_self,
    wk_self,
    wv_self,
    wo_self,
    wq_cross,
    wk_cross,
    wv_cross,
    wo_cross,
    w_gate,
    w_up,
    w_down,
    norm_scales,
    rel_bias,
):
    W = wq_self.shape[1]
    FFL = w_gate.shape[1]
    D = layer_in.shape[1]
    RL = layer_in.shape[0]
    heads = W // DH
    t_index = lax.axis_index("tensor")
    indicator = jnp.asarray(distance_indicator())
    base_row = jnp.einsum("bm,bh->hm", indicator, rel_bias, precision=lax.Precision.HIGHEST)
    base = jnp.stack([jnp.roll(base_row, s, axis=1) for s in range(8)], axis=1)

    first = gather_weights(wq_self, wk_self, wv_self, norm_scales.T)
    rows_all = spread(jnp.concatenate([layer_in, encoder_states, grad_out], axis=1))
    second = gather_weights(wo_self.T, wq_cross, wk_cross, wv_cross, wo_cross.T)
    third = gather_weights(w_gate, w_up, w_down.T)
    self_qkv_w = first[:, :3 * W]
    gains = first[:, 3 * W:].T.astype(F32)
    self_out_t = second[:, :W]
    cross_q_w = second[:, W:2 * W]
    cross_kv_w = second[:, 2 * W:4 * W]
    cross_out_t = second[:, 4 * W:]
    gate_up_w = third[:, :2 * FFL]
    down_t = third[:, 2 * FFL:]

    stream_all = rows_all[:, :D]
    source_rows = rows_all[:, D:2 * D]
    grad_rows = rows_all[:, 2 * D:]
    rows_one = to_half(unit_norm(stream_all.astype(F32))[0] * gains[0:1])
    stream_in = layer_in.astype(F32)
    unit_one, inverse_one = unit_norm(stream_in)

    self_qkv = to_half(matmul(rows_one, self_qkv_w))
    mixed_self, probs_self = attend(self_qkv, base, keep[0])
    stream_one = stream_in + collect(right_contract(mixed_self, self_out_t))
    unit_two, inverse_two = unit_norm(stream_one)
    rows_two = spread(to_half(unit_two * gains[1:2]))
    cross_qkv = jnp.concatenate(
        [to_half(matmul(rows_two, cross_q_w)), to_half(matmul(source_rows, cross_kv_w))], axis=1
    )
    mixed_cross, probs_cross = attend(cross_qkv, None, None)
    stream_two = stream_one + collect(right_contract(mixed_cross, cross_out_t))
    unit_three, inverse_three = unit_norm(stream_two)
    rows_three = spread(to_half(unit_three * gains[2:3]))
    gate_up = matmul(rows_three, gate_up_w)
    up_rows = gate_up[:, FFL:]
    activated, slope = gelu_pair(gate_up[:, :FFL])
    hidden = to_half(activated * up_rows)
    grad_hidden = matmul(grad_rows, down_t)
    grad_gate_up = to_half(
        jnp.concatenate([grad_hidden * up_rows * slope, grad_hidden * activated], axis=1)
    )
    grad_normed_three = collect(right_contract(grad_gate_up, gate_up_w))
    layer_out = to_half(stream_two + collect(right_contract(hidden, down_t)))
    grad_third = scatter_grads(
        left_contract(rows_three, grad_gate_up), left_contract(grad_rows, hidden)
    )
    back_three, gain_three = norm_backward(grad_normed_three, unit_three, inverse_three, gains[2:3])
    grad_stream_two = grad_out.astype(F32) + back_three
    grad_two_rows = spread(to_half(grad_stream_two))
    grad_mixed_cross = to_half(matmul(grad_two_rows, cross_out_t))
    grad_cross = attend_back(cross_qkv, probs_cross, grad_mixed_cross, False)
    grad_q_cross = grad_cross[:, :W]
    grad_kv_cross = grad_cross[:, W:]
    grad_normed_two = collect(right_contract(grad_q_cross, cross_q_w))
    grad_encoder = collect(right_contract(grad_kv_cross, cross_kv_w))
    grad_second = scatter_grads(
        left_contract(rows_two, grad_q_cross),
        left_contract(source_rows, grad_kv_cross),
        left_contract(grad_two_rows, mixed_cross),
    )
    back_two, gain_two = norm_backward(grad_normed_two, unit_two, inverse_two, gains[1:2])
    grad_stream_one = grad_stream_two + back_two
    grad_one_rows = spread(to_half(grad_stream_one))
    grad_mixed_self = to_half(matmul(grad_one_rows, self_out_t))
    grad_self, diagonal = attend_back(self_qkv, probs_self, grad_mixed_self, True)
    grad_normed_one = collect(right_contract(grad_self, self_qkv_w))
    grad_first = scatter_grads(
        left_contract(rows_one, grad_self), left_contract(grad_one_rows, mixed_self)
    )
    back_one, gain_one = norm_backward(grad_normed_one, unit_one, inverse_one, gains[0:1])
    grad_in = grad_stream_one + back_one

    bias_part = jnp.einsum("bm,hm->bh", indicator, diagonal, precision=lax.Precision.HIGHEST)
    tensor_size = lax.axis_size("tensor")
    bias_wide = jnp.where(
        (jnp.arange(tensor_size) == t_index)[:, None], bias_part.reshape(1, -1), 0.0
    )
    small = jnp.concatenate(
        [jnp.stack([gain_one, gain_two, gain_three]).reshape(-1), bias_wide.reshape(-1)]
    )
    small = lax.psum(small, ("dp", "tensor"))
    share = D // (lax.axis_size("dp") * tensor_size)
    place = lax.axis_index("dp") * tensor_size + t_index
    grad_norm_scales = lax.dynamic_slice_in_dim(small[:3 * D].reshape(3, D), place * share, share, 1)
    grad_rel_bias = lax.dynamic_slice_in_dim(
        small[3 * D:].reshape(tensor_size, NBUCKET, heads), t_index, 1, 0
    )[0]
    return (
        layer_out,
        grad_in,
        grad_encoder,
        grad_first[:, :W],
        grad_first[:, W:2 * W],
        grad_first[:, 2 * W:3 * W],
        grad_first[:, 3 * W:].T,
        grad_second[:, :W],
        grad_second[:, W:2 * W],
        grad_second[:, 2 * W:3 * W],
        grad_second[:, 3 * W:].T,
        grad_third[:, :FFL],
        grad_third[:, FFL:2 * FFL],
        grad_third[:, 2 * FFL:].T,
        grad_norm_scales,
        grad_rel_bias,
    )


def solution(mesh):
    in_specs = (
        P(("dp", "tensor"), None),
        P(("dp", "tensor"), None),
        P(("dp", "tensor"), None),
        P("dp", None, None),
        P("dp", None, None),
        P("dp", "tensor"),
        P("dp", "tensor"),
        P("dp", "tensor"),
        P("tensor", "dp"),
        P("dp", "tensor"),
        P("dp", "tensor"),
        P("dp", "tensor"),
        P("tensor", "dp"),
        P("dp", "tensor"),
        P("dp", "tensor"),
        P("tensor", "dp"),
        P(None, "dp"),
        P(None, "tensor"),
    )
    out_specs = (
        P(("dp", "tensor"), None),
        P(("dp", "tensor"), None),
        P(("dp", "tensor"), None),
        P("dp", "tensor"),
        P("dp", "tensor"),
        P("dp", "tensor"),
        P("tensor", "dp"),
        P("dp", "tensor"),
        P("dp", "tensor"),
        P("dp", "tensor"),
        P("tensor", "dp"),
        P("dp", "tensor"),
        P("dp", "tensor"),
        P("tensor", "dp"),
        P(None, ("dp", "tensor")),
        P(None, "tensor"),
    )
    return jax.shard_map(
        per_device, mesh=mesh, in_specs=in_specs, out_specs=out_specs, check_vma=False
    )
```

```python
import math

import jax
import jax.numpy as jnp
import numpy as np
from jax import lax
from jax.experimental import pallas as pl
from jax.experimental.pallas import tpu as pltpu
from jax.sharding import PartitionSpec as P

DH = 64
NBUCKET = 32
L = 512
BLOCK = 128
NORM_EPSILON = 1e-06
MASKED_SCORE = -1e30
GELU_CUBIC = 0.044715
F32 = jnp.float32
BF16 = jnp.bfloat16


def to_half(values):
    return values.astype(BF16)


def matmul(left_side, right_side):
    return jnp.dot(left_side, right_side, preferred_element_type=F32)


def left_contract(left_side, right_side):
    return lax.dot_general(left_side, right_side, (((0,), (0,)), ((), ())), preferred_element_type=F32)


def right_contract(left_side, right_side):
    return lax.dot_general(left_side, right_side, (((1,), (1,)), ((), ())), preferred_element_type=F32)


def gelu_pair(values):
    root_scale = math.sqrt(2.0 / math.pi)
    interior = root_scale * (values + GELU_CUBIC * values * values * values)
    tangent = jnp.tanh(interior)
    activated = 0.5 * values * (1.0 + tangent)
    slope = 0.5 * (1.0 + tangent) + 0.5 * values * (1.0 - tangent * tangent) * root_scale * (
        1.0 + 3.0 * GELU_CUBIC * values * values
    )
    return (activated, slope)


def unit_norm(stream):
    inverse = lax.rsqrt(jnp.mean(stream * stream, axis=-1, keepdims=True) + NORM_EPSILON)
    return (stream * inverse, inverse)


def norm_backward(incoming, unit_rows, inverse, gain):
    scaled = incoming * gain
    result = inverse * (scaled - unit_rows * jnp.mean(scaled * unit_rows, axis=-1, keepdims=True))
    return (result, jnp.sum(incoming * unit_rows, axis=0))


def spread(rows_local):
    return lax.all_gather(rows_local, "tensor", axis=0, tiled=True)


def collect(partial_rows):
    return lax.psum_scatter(to_half(partial_rows), "tensor", scatter_dimension=0, tiled=True).astype(F32)


def distance_indicator():
    exact = NBUCKET // 2
    distance = (-np.arange(L)) % L
    log_part = exact + np.floor(
        np.log(np.maximum(distance, 1) / exact) / np.log(128 / exact) * (NBUCKET - exact)
    ).astype(np.int64)
    bucket = np.where(distance < exact, distance, np.minimum(log_part, NBUCKET - 1))
    return (bucket[None, :] == np.arange(NBUCKET)[:, None]).astype(np.float32)


def whole(*shape_and_type):
    return jax.ShapeDtypeStruct(*shape_and_type)


def call(kernel, outs, scratch=(), name=None):
    return pl.pallas_call(
        kernel,
        out_shape=outs,
        scratch_shapes=list(scratch),
        name=name,
        compiler_params=pltpu.CompilerParams(vmem_limit_bytes=60 * 1024 * 1024),
    )


def attend_block(q, k, v, bias, allowed):
    logits = right_contract(q, k)
    if bias is not None:
        logits = jnp.where(allowed, logits + bias, MASKED_SCORE)
    row_max = jnp.max(logits, axis=-1, keepdims=True)
    powers = jnp.exp(logits - row_max)
    probs = to_half(powers / jnp.sum(powers, axis=-1, keepdims=True))
    return probs, to_half(matmul(probs, v))


def attend_kernel(masked, qkv_ref, *refs):
    if masked:
        base_ref, keep_ref, mixed_ref, probs_ref = refs
    else:
        mixed_ref, probs_ref = refs
    width = mixed_ref.shape[1]
    heads = width // DH
    for block in range(L // BLOCK):
        rows = slice(block * BLOCK, (block + 1) * BLOCK)
        reach = (block + 1) * BLOCK if masked else L
        allowed = keep_ref[rows, :reach] == 1 if masked else None
        pieces = []
        for h in range(heads):
            bias = None
            if masked:
                base = base_ref[h]
                tiles = [
                    pltpu.roll(base, 8 * t, 1) if t else base
                    for t in range(block * BLOCK // 8, (block + 1) * BLOCK // 8)
                ]
                bias = jnp.concatenate(tiles, axis=0)[:, :reach]
            probs, mixed = attend_block(
                qkv_ref[rows, h * DH:(h + 1) * DH],
                qkv_ref[:reach, width + h * DH:width + (h + 1) * DH],
                qkv_ref[:reach, 2 * width + h * DH:2 * width + (h + 1) * DH],
                bias,
                allowed,
            )
            probs_ref[h, rows, :reach] = probs
            pieces.append(mixed)
        mixed_ref[rows, :] = jnp.concatenate(pieces, axis=1)


def attend_back_kernel(masked, qkv_ref, probs_ref, gm_ref, grad_ref, *refs):
    if masked:
        diag_ref, key_total, value_total = refs
    else:
        key_total, value_total = refs
    width = gm_ref.shape[1]
    heads = width // DH
    for h in range(heads):
        cq = slice(h * DH, (h + 1) * DH)
        ck = slice(width + h * DH, width + (h + 1) * DH)
        cv = slice(2 * width + h * DH, 2 * width + (h + 1) * DH)
        diag = jnp.zeros((8, L), F32)
        for block in reversed(range(L // BLOCK)):
            rows = slice(block * BLOCK, (block + 1) * BLOCK)
            reach = (block + 1) * BLOCK if masked else L
            probs = probs_ref[h, rows, :reach]
            gm = gm_ref[rows, cq]
            grad_probs = right_contract(gm, qkv_ref[:reach, cv])
            probs_full = probs.astype(F32)
            centre = jnp.sum(probs_full * grad_probs, axis=-1, keepdims=True)
            grad_logits = probs_full * (grad_probs - centre)
            half = to_half(grad_logits)
            grad_ref[rows, cq] = to_half(matmul(half, qkv_ref[:reach, ck]))
            key_part = left_contract(half, qkv_ref[rows, cq])
            value_part = left_contract(probs, gm)
            if block == L // BLOCK - 1:
                key_total[:, :] = key_part
                value_total[:, :] = value_part
            else:
                key_total[:reach, :] += key_part
                value_total[:reach, :] += value_part
            if masked:
                for t in range(BLOCK // 8):
                    tile = grad_logits[8 * t:8 * t + 8]
                    if reach < L:
                        tile = jnp.concatenate([tile, jnp.zeros((8, L - reach), F32)], axis=1)
                    shift = (L - (block * BLOCK + 8 * t)) % L
                    diag = diag + (pltpu.roll(tile, shift, 1) if shift else tile)
        grad_ref[:, ck] = to_half(key_total[...])
        grad_ref[:, cv] = to_half(value_total[...])
        if masked:
            total = diag[0:1]
            for s in range(1, 8):
                total = total + pltpu.roll(diag[s:s + 1], L - s, 1)
            diag_ref[h:h + 1, :] = total


MESH = pl.DeviceIdType.MESH


def tensor_place():
    me = lax.axis_index("tensor")
    partner = me + 1 - 2 * lax.rem(me, 2)
    across = lax.rem(me + 2, 4)
    return me, partner, across


def greet(*peers):
    barrier = pltpu.get_barrier_semaphore()
    for peer in peers:
        pl.semaphore_signal(barrier, inc=1, device_id=peer, device_id_type=MESH)
    pl.semaphore_wait(barrier, len(peers))


def remote(source, target, sems, index, peer):
    copy = pltpu.make_async_remote_copy(
        src_ref=source,
        dst_ref=target,
        send_sem=sems[0].at[index],
        recv_sem=sems[1].at[index],
        device_id={"tensor": peer},
        device_id_type=MESH,
    )
    copy.start()
    return copy


def reduce_rows(lhs_ref, w_ref, sent, landed, sems):
    me, partner, across = tensor_place()
    share = landed.shape[1]

    def part(block):
        return right_contract(lhs_ref[pl.ds(pl.multiple_of(block * share, share), share), :], w_ref[...])

    sent[0] = to_half(part(lax.rem(partner + 2, 4)))
    far = remote(sent.at[0], landed.at[0], sems, 0, partner)
    sent[1] = to_half(part(partner))
    near = remote(sent.at[1], landed.at[1], sems, 1, partner)
    mine_far = part(across)
    far.wait()
    sent[2] = to_half(mine_far + landed[0].astype(F32))
    over = remote(sent.at[2], landed.at[2], sems, 2, across)
    mine = part(me)
    near.wait()
    mine = mine + landed[1].astype(F32)
    over.wait()
    return mine + landed[2].astype(F32)


def spread_rows(rows, held, rows_ref, sems):
    me, partner, across = tensor_place()
    share = rows.shape[0]

    def block(index):
        return held.at[pl.ds(pl.multiple_of(index * share, share), share)]

    held[pl.ds(pl.multiple_of(me * share, share), share), :] = rows
    over = remote(block(me), block(me), sems, 3, across)
    near = remote(block(me), block(me), sems, 4, partner)
    over.wait()
    forward = remote(block(across), block(across), sems, 5, partner)
    near.wait()
    forward.wait()
    rows_ref[...] = held[...]


def forward_kernel(lhs_ref, w_ref, stream_ref, gain_ref, rows_ref, out_ref, sent, landed, held, send, recv):
    me, partner, across = tensor_place()
    greet({"tensor": partner}, {"tensor": across})
    stream = stream_ref[...].astype(F32) + reduce_rows(lhs_ref, w_ref, sent, landed, (send, recv))
    out_ref[...] = stream
    spread_rows(to_half(unit_norm(stream)[0] * gain_ref[...]), held, rows_ref, (send, recv))


def backward_kernel(spreading, lhs_ref, w_ref, stream_ref, grad_ref, gain_ref, *refs):
    if spreading:
        rows_ref, out_ref, gain_out, sent, landed, held, send, recv = refs
    else:
        out_ref, gain_out, sent, landed, send, recv = refs
    me, partner, across = tensor_place()
    greet({"tensor": partner}, {"tensor": across})
    unit, inverse = unit_norm(stream_ref[...].astype(F32))
    incoming = reduce_rows(lhs_ref, w_ref, sent, landed, (send, recv))
    back, gain_grad = norm_backward(incoming, unit, inverse, gain_ref[...])
    grad = grad_ref[...].astype(F32) + back
    out_ref[...] = grad
    gain_out[...] = gain_grad[None]
    if spreading:
        spread_rows(to_half(grad), held, rows_ref, (send, recv))


def exchange(kernel, number, outs, share, width, rows, *operands):
    count = 6 if rows else 3
    scratch = [pltpu.VMEM((3, share, width), BF16), pltpu.VMEM((3, share, width), BF16)]
    if rows:
        scratch.append(pltpu.VMEM((rows, width), BF16))
    scratch += [pltpu.SemaphoreType.DMA((count,)), pltpu.SemaphoreType.DMA((count,))]
    return pl.pallas_call(
        kernel,
        out_shape=outs,
        scratch_shapes=scratch,
        name=f"exchange_{number}",
        compiler_params=pltpu.CompilerParams(
            collective_id=number, has_side_effects=True, vmem_limit_bytes=60 * 1024 * 1024
        ),
    )(*operands)


def forward_exchange(number, lhs, w, stream, gain):
    share, width = stream.shape
    outs = (whole((L, width), BF16), whole((share, width), F32))
    return exchange(forward_kernel, number, outs, share, width, L, lhs, w, stream, gain)


def backward_exchange(number, spreading, lhs, w, stream, grad, gain):
    share, width = stream.shape
    outs = (whole((share, width), F32), whole((1, width), F32))
    if spreading:
        outs = (whole((L, width), BF16),) + outs

    def kernel(*refs):
        backward_kernel(spreading, *refs)

    return exchange(
        kernel, number, outs, share, width, L if spreading else 0, lhs, w, stream, grad, gain
    )


def sum_kernel(grads_ref, small_ref, out_ref, small_out, landed, small_landed, small_sum, gain_landed, *sems):
    send, recv, small_send, small_recv, gain_send, gain_recv = sems
    n = grads_ref.shape[0]
    me = lax.axis_index("dp")
    column = lax.axis_index("tensor")
    barrier = pltpu.get_barrier_semaphore()

    def hello(o, carry):
        pl.semaphore_signal(barrier, inc=1, device_id={"dp": lax.rem(me + o, n)}, device_id_type=MESH)
        return carry

    lax.fori_loop(1, n, hello, 0)
    for o in range(1, 4):
        pl.semaphore_signal(barrier, inc=1, device_id={"tensor": lax.rem(column + o, 4)}, device_id_type=MESH)
    pl.semaphore_wait(barrier, n - 1 + 3)

    def copies(o):
        peer = lax.rem(me + o, n)
        big = pltpu.make_async_remote_copy(
            src_ref=grads_ref.at[peer],
            dst_ref=landed.at[o],
            send_sem=send.at[o],
            recv_sem=recv.at[o],
            device_id={"dp": peer},
            device_id_type=MESH,
        )
        little = pltpu.make_async_remote_copy(
            src_ref=small_ref.at[peer],
            dst_ref=small_landed.at[o],
            send_sem=small_send.at[o],
            recv_sem=small_recv.at[o],
            device_id={"dp": peer},
            device_id_type=MESH,
        )
        return big, little

    def launch_small(o, carry):
        copies(o)[1].start()
        return carry

    def launch(o, carry):
        copies(o)[0].start()
        return carry

    def finish_small(o, total):
        copies(o)[1].wait()
        return total + small_landed[o]

    lax.fori_loop(1, n, launch_small, 0)
    lax.fori_loop(1, n, launch, 0)
    small = lax.fori_loop(1, n, finish_small, small_ref[me])
    small_sum[...] = small
    gain_copies = []
    for o in range(1, 4):
        copy = pltpu.make_async_remote_copy(
            src_ref=small_sum,
            dst_ref=gain_landed.at[o],
            send_sem=gain_send.at[o],
            recv_sem=gain_recv.at[o],
            device_id={"tensor": lax.rem(column + o, 4)},
            device_id_type=MESH,
        )
        copy.start()
        gain_copies.append(copy)
    small_out[0] = small
    for o, copy in enumerate(gain_copies, 1):
        copy.wait()
        small = small + gain_landed[o]
    small_out[1] = small
    out_ref[...] = grads_ref[me].astype(F32)

    def finish(o, carry):
        copies(o)[0].wait()
        out_ref[...] += landed[o].astype(F32)
        return carry

    lax.fori_loop(1, n, finish, 0)


def sum_over_dp(number, grads, small):
    n, rows, width = grads.shape
    dma = pltpu.SemaphoreType.DMA
    return pl.pallas_call(
        sum_kernel,
        out_shape=(whole((rows, width), F32), whole((2,) + small.shape[1:], F32)),
        scratch_shapes=[
            pltpu.VMEM(grads.shape, BF16),
            pltpu.VMEM(small.shape, F32),
            pltpu.VMEM(small.shape[1:], F32),
            pltpu.VMEM((4,) + small.shape[1:], F32),
            dma((n,)),
            dma((n,)),
            dma((n,)),
            dma((n,)),
            dma((4,)),
            dma((4,)),
        ],
        name="sum_over_dp",
        compiler_params=pltpu.CompilerParams(
            collective_id=number, has_side_effects=True, vmem_limit_bytes=60 * 1024 * 1024
        ),
    )(grads, small)


def attend(qkv, base, keep):
    width = qkv.shape[1] // 3
    outs = (
        whole((L, width), BF16),
        whole((width // DH, L, L), BF16),
    )
    if base is None:
        return call(lambda *r: attend_kernel(False, *r), outs, name="cross_fwd")(qkv)
    return call(lambda *r: attend_kernel(True, *r), outs, name="self_fwd")(qkv, base, keep)


def attend_back(qkv, probs, grad_mixed, masked):
    width = qkv.shape[1] // 3
    scratch = (pltpu.VMEM((L, DH), F32), pltpu.VMEM((L, DH), F32))
    grads = whole((L, 3 * width), BF16)
    if masked:
        return call(
            lambda *r: attend_back_kernel(True, *r),
            (grads, whole((width // DH, L), F32)),
            scratch,
            name="self_bwd",
        )(qkv, probs, grad_mixed)
    return call(lambda *r: attend_back_kernel(False, *r), grads, scratch, name="cross_bwd")(
        qkv, probs, grad_mixed
    )


def gather_weights(*parts):
    return lax.all_gather(jnp.concatenate(parts, axis=1), "dp", axis=0, tiled=True)


def scatter_grads(*parts):
    return lax.psum_scatter(to_half(jnp.concatenate(parts, axis=1)), "dp", scatter_dimension=0, tiled=True).astype(F32)


def per_device(
    layer_in,
    encoder_states,
    grad_out,
    buckets,
    keep,
    wq_self,
    wk_self,
    wv_self,
    wo_self,
    wq_cross,
    wk_cross,
    wv_cross,
    wo_cross,
    w_gate,
    w_up,
    w_down,
    norm_scales,
    rel_bias,
):
    W = wq_self.shape[1]
    FFL = w_gate.shape[1]
    D = layer_in.shape[1]
    heads = W // DH
    t_index = lax.axis_index("tensor")
    indicator = jnp.asarray(distance_indicator())
    base_row = jnp.einsum("bm,bh->hm", indicator, rel_bias, precision=lax.Precision.HIGHEST)
    base = jnp.stack([jnp.roll(base_row, s, axis=1) for s in range(8)], axis=1)

    first = gather_weights(
        wq_self, wk_self, wv_self, wo_self.T, wq_cross, wk_cross, wv_cross, wo_cross.T, norm_scales.T
    )
    stream_all = spread(layer_in)
    others = spread(jnp.concatenate([encoder_states, grad_out], axis=1))
    second = gather_weights(w_gate, w_up, w_down.T)
    self_qkv_w = first[:, :3 * W]
    self_out_t = first[:, 3 * W:4 * W]
    cross_q_w = first[:, 4 * W:5 * W]
    cross_kv_w = first[:, 5 * W:7 * W]
    cross_out_t = first[:, 7 * W:8 * W]
    gains = first[:, 8 * W:].T.astype(F32)
    gate_up_w = second[:, :2 * FFL]
    down_t = second[:, 2 * FFL:]
    source_rows = others[:, :D]
    grad_rows = others[:, D:]

    rows_one = to_half(unit_norm(stream_all.astype(F32))[0] * gains[0:1])
    self_qkv = to_half(matmul(rows_one, self_qkv_w))
    mixed_self, probs_self = attend(self_qkv, base, keep[0])
    rows_two, stream_one = forward_exchange(1, mixed_self, self_out_t, layer_in, gains[1:2])
    cross_qkv = jnp.concatenate(
        [to_half(matmul(rows_two, cross_q_w)), to_half(matmul(source_rows, cross_kv_w))], axis=1
    )
    mixed_cross, probs_cross = attend(cross_qkv, None, None)
    rows_three, stream_two = forward_exchange(2, mixed_cross, cross_out_t, stream_one, gains[2:3])
    gate_up = matmul(rows_three, gate_up_w)
    up_rows = gate_up[:, FFL:]
    activated, slope = gelu_pair(gate_up[:, :FFL])
    hidden = to_half(activated * up_rows)
    grad_hidden = matmul(grad_rows, down_t)
    grad_gate_up = to_half(
        jnp.concatenate([grad_hidden * up_rows * slope, grad_hidden * activated], axis=1)
    )
    grad_two_rows, grad_stream_two, gain_three = backward_exchange(
        3, True, grad_gate_up, gate_up_w, stream_two, grad_out, gains[2:3]
    )
    grad_third = scatter_grads(
        left_contract(rows_three, grad_gate_up), left_contract(grad_rows, hidden)
    )
    layer_out = to_half(stream_two + collect(right_contract(hidden, down_t)))
    grad_mixed_cross = to_half(matmul(grad_two_rows, cross_out_t))
    grad_cross = attend_back(cross_qkv, probs_cross, grad_mixed_cross, False)
    grad_q_cross = grad_cross[:, :W]
    grad_kv_cross = grad_cross[:, W:]
    grad_one_rows, grad_stream_one, gain_two = backward_exchange(
        4, True, grad_q_cross, cross_q_w, stream_one, grad_stream_two, gains[1:2]
    )
    grad_encoder = collect(right_contract(grad_kv_cross, cross_kv_w))
    grad_mixed_self = to_half(matmul(grad_one_rows, self_out_t))
    grad_self, diagonal = attend_back(self_qkv, probs_self, grad_mixed_self, True)
    grad_in, gain_one = backward_exchange(
        5, False, grad_self, self_qkv_w, layer_in, grad_stream_one, gains[0:1]
    )
    bias_part = jnp.einsum("bm,hm->bh", indicator, diagonal, precision=lax.Precision.HIGHEST)
    dp_size = lax.axis_size("dp")
    tensor_size = lax.axis_size("tensor")
    share = D // dp_size
    grads = jnp.concatenate(
        [
            to_half(part)
            for part in (
                left_contract(rows_one, grad_self),
                left_contract(grad_one_rows, mixed_self),
                left_contract(rows_two, grad_q_cross),
                left_contract(source_rows, grad_kv_cross),
                left_contract(grad_two_rows, mixed_cross),
            )
        ],
        axis=1,
    ).reshape(dp_size, share, 8 * W)
    gain_part = jnp.concatenate([gain_one, gain_two, gain_three]).reshape(3, dp_size, share)
    small = jnp.concatenate(
        [
            jnp.pad(gain_part.transpose(1, 0, 2), ((0, 0), (0, 0), (0, 128 - share))),
            jnp.broadcast_to(
                jnp.pad(bias_part.reshape(1, 1, -1), ((0, 0), (0, 0), (0, 128 - NBUCKET * heads))),
                (dp_size, 1, 128),
            ),
            jnp.zeros((dp_size, 4, 128), F32),
        ],
        axis=1,
    )
    summed, small_sums = sum_over_dp(6, grads, small)
    grad_first = summed[:, :4 * W]
    grad_second = summed[:, 4 * W:]
    own = share // tensor_size
    grad_norm_scales = lax.dynamic_slice_in_dim(small_sums[1, :3], t_index * own, own, 1)
    grad_rel_bias = small_sums[0, 3, :NBUCKET * heads].reshape(NBUCKET, heads)
    return (
        layer_out,
        grad_in,
        grad_encoder,
        grad_first[:, :W],
        grad_first[:, W:2 * W],
        grad_first[:, 2 * W:3 * W],
        grad_first[:, 3 * W:].T,
        grad_second[:, :W],
        grad_second[:, W:2 * W],
        grad_second[:, 2 * W:3 * W],
        grad_second[:, 3 * W:].T,
        grad_third[:, :FFL],
        grad_third[:, FFL:2 * FFL],
        grad_third[:, 2 * FFL:].T,
        grad_norm_scales,
        grad_rel_bias,
    )


def solution(mesh):
    in_specs = (
        P(("dp", "tensor"), None),
        P(("dp", "tensor"), None),
        P(("dp", "tensor"), None),
        P("dp", None, None),
        P("dp", None, None),
        P("dp", "tensor"),
        P("dp", "tensor"),
        P("dp", "tensor"),
        P("tensor", "dp"),
        P("dp", "tensor"),
        P("dp", "tensor"),
        P("dp", "tensor"),
        P("tensor", "dp"),
        P("dp", "tensor"),
        P("dp", "tensor"),
        P("tensor", "dp"),
        P(None, "dp"),
        P(None, "tensor"),
    )
    out_specs = (
        P(("dp", "tensor"), None),
        P(("dp", "tensor"), None),
        P(("dp", "tensor"), None),
        P("dp", "tensor"),
        P("dp", "tensor"),
        P("dp", "tensor"),
        P("tensor", "dp"),
        P("dp", "tensor"),
        P("dp", "tensor"),
        P("dp", "tensor"),
        P("tensor", "dp"),
        P("dp", "tensor"),
        P("dp", "tensor"),
        P("tensor", "dp"),
        P(None, ("dp", "tensor")),
        P(None, "tensor"),
    )
    return jax.shard_map(
        per_device, mesh=mesh, in_specs=in_specs, out_specs=out_specs, check_vma=False
    )
```

```python
import math

import jax
import jax.numpy as jnp
import numpy as np
from jax import lax
from jax.experimental import pallas as pl
from jax.experimental.pallas import tpu as pltpu
from jax.sharding import PartitionSpec as P

DH = 64
NBUCKET = 32
L = 512
BLOCK = 128
NORM_EPSILON = 1e-06
MASKED_SCORE = -1e30
GELU_CUBIC = 0.044715
F32 = jnp.float32
BF16 = jnp.bfloat16


def to_half(values):
    return values.astype(BF16)


def matmul(left_side, right_side):
    return jnp.dot(left_side, right_side, preferred_element_type=F32)


def left_contract(left_side, right_side):
    return lax.dot_general(left_side, right_side, (((0,), (0,)), ((), ())), preferred_element_type=F32)


def right_contract(left_side, right_side):
    return lax.dot_general(left_side, right_side, (((1,), (1,)), ((), ())), preferred_element_type=F32)


def gelu_pair(values):
    root_scale = math.sqrt(2.0 / math.pi)
    interior = root_scale * (values + GELU_CUBIC * values * values * values)
    tangent = jnp.tanh(interior)
    activated = 0.5 * values * (1.0 + tangent)
    slope = 0.5 * (1.0 + tangent) + 0.5 * values * (1.0 - tangent * tangent) * root_scale * (
        1.0 + 3.0 * GELU_CUBIC * values * values
    )
    return (activated, slope)


def unit_norm(stream):
    inverse = lax.rsqrt(jnp.mean(stream * stream, axis=-1, keepdims=True) + NORM_EPSILON)
    return (stream * inverse, inverse)


def norm_backward(incoming, unit_rows, inverse, gain):
    scaled = incoming * gain
    result = inverse * (scaled - unit_rows * jnp.mean(scaled * unit_rows, axis=-1, keepdims=True))
    return (result, jnp.sum(incoming * unit_rows, axis=0))


def spread(rows_local):
    return lax.all_gather(rows_local, "tensor", axis=0, tiled=True)


def collect(partial_rows):
    return lax.psum_scatter(to_half(partial_rows), "tensor", scatter_dimension=0, tiled=True).astype(F32)


def distance_indicator():
    exact = NBUCKET // 2
    distance = (-np.arange(L)) % L
    log_part = exact + np.floor(
        np.log(np.maximum(distance, 1) / exact) / np.log(128 / exact) * (NBUCKET - exact)
    ).astype(np.int64)
    bucket = np.where(distance < exact, distance, np.minimum(log_part, NBUCKET - 1))
    return (bucket[None, :] == np.arange(NBUCKET)[:, None]).astype(np.float32)


def whole(*shape_and_type):
    return jax.ShapeDtypeStruct(*shape_and_type)


def call(kernel, outs, scratch=(), name=None):
    return pl.pallas_call(
        kernel,
        out_shape=outs,
        scratch_shapes=list(scratch),
        name=name,
        compiler_params=pltpu.CompilerParams(vmem_limit_bytes=60 * 1024 * 1024),
    )


def attend_block(q, k, v, bias, allowed):
    logits = right_contract(q, k)
    if bias is not None:
        logits = jnp.where(allowed, logits + bias, MASKED_SCORE)
    row_max = jnp.max(logits, axis=-1, keepdims=True)
    powers = jnp.exp(logits - row_max)
    probs = to_half(powers / jnp.sum(powers, axis=-1, keepdims=True))
    return probs, to_half(matmul(probs, v))


def attend_kernel(masked, qkv_ref, *refs):
    if masked:
        base_ref, keep_ref, mixed_ref, probs_ref = refs
    else:
        mixed_ref, probs_ref = refs
    width = mixed_ref.shape[1]
    heads = width // DH
    for block in range(L // BLOCK):
        rows = slice(block * BLOCK, (block + 1) * BLOCK)
        reach = (block + 1) * BLOCK if masked else L
        allowed = keep_ref[rows, :reach] == 1 if masked else None
        pieces = []
        for h in range(heads):
            bias = None
            if masked:
                base = base_ref[h]
                tiles = [
                    pltpu.roll(base, 8 * t, 1) if t else base
                    for t in range(block * BLOCK // 8, (block + 1) * BLOCK // 8)
                ]
                bias = jnp.concatenate(tiles, axis=0)[:, :reach]
            probs, mixed = attend_block(
                qkv_ref[rows, h * DH:(h + 1) * DH],
                qkv_ref[:reach, width + h * DH:width + (h + 1) * DH],
                qkv_ref[:reach, 2 * width + h * DH:2 * width + (h + 1) * DH],
                bias,
                allowed,
            )
            probs_ref[h, rows, :reach] = probs
            pieces.append(mixed)
        mixed_ref[rows, :] = jnp.concatenate(pieces, axis=1)


def attend_back_kernel(masked, qkv_ref, probs_ref, gm_ref, grad_ref, *refs):
    if masked:
        diag_ref, key_total, value_total = refs
    else:
        key_total, value_total = refs
    width = gm_ref.shape[1]
    heads = width // DH
    for h in range(heads):
        cq = slice(h * DH, (h + 1) * DH)
        ck = slice(width + h * DH, width + (h + 1) * DH)
        cv = slice(2 * width + h * DH, 2 * width + (h + 1) * DH)
        diag = jnp.zeros((8, L), F32)
        for block in reversed(range(L // BLOCK)):
            rows = slice(block * BLOCK, (block + 1) * BLOCK)
            reach = (block + 1) * BLOCK if masked else L
            probs = probs_ref[h, rows, :reach]
            gm = gm_ref[rows, cq]
            grad_probs = right_contract(gm, qkv_ref[:reach, cv])
            probs_full = probs.astype(F32)
            centre = jnp.sum(probs_full * grad_probs, axis=-1, keepdims=True)
            grad_logits = probs_full * (grad_probs - centre)
            half = to_half(grad_logits)
            grad_ref[rows, cq] = to_half(matmul(half, qkv_ref[:reach, ck]))
            key_part = left_contract(half, qkv_ref[rows, cq])
            value_part = left_contract(probs, gm)
            if block == L // BLOCK - 1:
                key_total[:, :] = key_part
                value_total[:, :] = value_part
            else:
                key_total[:reach, :] += key_part
                value_total[:reach, :] += value_part
            if masked:
                for t in range(BLOCK // 8):
                    tile = grad_logits[8 * t:8 * t + 8]
                    if reach < L:
                        tile = jnp.concatenate([tile, jnp.zeros((8, L - reach), F32)], axis=1)
                    shift = (L - (block * BLOCK + 8 * t)) % L
                    diag = diag + (pltpu.roll(tile, shift, 1) if shift else tile)
        grad_ref[:, ck] = to_half(key_total[...])
        grad_ref[:, cv] = to_half(value_total[...])
        if masked:
            total = diag[0:1]
            for s in range(1, 8):
                total = total + pltpu.roll(diag[s:s + 1], L - s, 1)
            diag_ref[h:h + 1, :] = total


MESH = pl.DeviceIdType.MESH


def tensor_place():
    me = lax.axis_index("tensor")
    partner = me + 1 - 2 * lax.rem(me, 2)
    across = lax.rem(me + 2, 4)
    return me, partner, across


def greet(*peers):
    barrier = pltpu.get_barrier_semaphore()
    for peer in peers:
        pl.semaphore_signal(barrier, inc=1, device_id=peer, device_id_type=MESH)
    pl.semaphore_wait(barrier, len(peers))


def remote(source, target, sems, index, peer):
    copy = pltpu.make_async_remote_copy(
        src_ref=source,
        dst_ref=target,
        send_sem=sems[0].at[index],
        recv_sem=sems[1].at[index],
        device_id={"tensor": peer},
        device_id_type=MESH,
    )
    copy.start()
    return copy


def reduce_rows(lhs_ref, w_ref, sent, landed, sems):
    me, partner, across = tensor_place()
    share = landed.shape[1]

    def part(block):
        return right_contract(lhs_ref[pl.ds(pl.multiple_of(block * share, share), share), :], w_ref[...])

    sent[0] = to_half(part(lax.rem(partner + 2, 4)))
    far = remote(sent.at[0], landed.at[0], sems, 0, partner)
    sent[1] = to_half(part(partner))
    near = remote(sent.at[1], landed.at[1], sems, 1, partner)
    mine_far = part(across)
    far.wait()
    sent[2] = to_half(mine_far + landed[0].astype(F32))
    over = remote(sent.at[2], landed.at[2], sems, 2, across)
    mine = part(me)
    near.wait()
    mine = mine + landed[1].astype(F32)
    over.wait()
    return mine + landed[2].astype(F32)


def spread_rows(rows, held, rows_ref, sems):
    me, partner, across = tensor_place()
    share = rows.shape[0]

    def block(index):
        return held.at[pl.ds(pl.multiple_of(index * share, share), share)]

    held[pl.ds(pl.multiple_of(me * share, share), share), :] = rows
    over = remote(block(me), block(me), sems, 3, across)
    near = remote(block(me), block(me), sems, 4, partner)
    over.wait()
    forward = remote(block(across), block(across), sems, 5, partner)
    near.wait()
    forward.wait()
    rows_ref[...] = held[...]


def forward_kernel(lhs_ref, w_ref, stream_ref, gain_ref, rows_ref, out_ref, sent, landed, held, send, recv):
    me, partner, across = tensor_place()
    greet({"tensor": partner}, {"tensor": across})
    stream = stream_ref[...].astype(F32) + reduce_rows(lhs_ref, w_ref, sent, landed, (send, recv))
    out_ref[...] = stream
    spread_rows(to_half(unit_norm(stream)[0] * gain_ref[...]), held, rows_ref, (send, recv))


def backward_kernel(spreading, lhs_ref, w_ref, stream_ref, grad_ref, gain_ref, *refs):
    if spreading:
        rows_ref, out_ref, gain_out, sent, landed, held, send, recv = refs
    else:
        out_ref, gain_out, sent, landed, send, recv = refs
    me, partner, across = tensor_place()
    greet({"tensor": partner}, {"tensor": across})
    unit, inverse = unit_norm(stream_ref[...].astype(F32))
    incoming = reduce_rows(lhs_ref, w_ref, sent, landed, (send, recv))
    back, gain_grad = norm_backward(incoming, unit, inverse, gain_ref[...])
    grad = grad_ref[...].astype(F32) + back
    out_ref[...] = grad
    gain_out[...] = gain_grad[None]
    if spreading:
        spread_rows(to_half(grad), held, rows_ref, (send, recv))


def exchange(kernel, number, outs, share, width, rows, *operands):
    count = 6 if rows else 3
    scratch = [pltpu.VMEM((3, share, width), BF16), pltpu.VMEM((3, share, width), BF16)]
    if rows:
        scratch.append(pltpu.VMEM((rows, width), BF16))
    scratch += [pltpu.SemaphoreType.DMA((count,)), pltpu.SemaphoreType.DMA((count,))]
    return pl.pallas_call(
        kernel,
        out_shape=outs,
        scratch_shapes=scratch,
        name=f"exchange_{number}",
        compiler_params=pltpu.CompilerParams(
            collective_id=number, has_side_effects=True, vmem_limit_bytes=60 * 1024 * 1024
        ),
    )(*operands)


def forward_exchange(number, lhs, w, stream, gain):
    share, width = stream.shape
    outs = (whole((L, width), BF16), whole((share, width), F32))
    return exchange(forward_kernel, number, outs, share, width, L, lhs, w, stream, gain)


def backward_exchange(number, spreading, lhs, w, stream, grad, gain):
    share, width = stream.shape
    outs = (whole((share, width), F32), whole((1, width), F32))
    if spreading:
        outs = (whole((L, width), BF16),) + outs

    def kernel(*refs):
        backward_kernel(spreading, *refs)

    return exchange(
        kernel, number, outs, share, width, L if spreading else 0, lhs, w, stream, grad, gain
    )


def sum_kernel(grads_ref, small_ref, out_ref, small_out, landed, small_landed, small_sum, gain_landed, *sems):
    send, recv, small_send, small_recv, gain_send, gain_recv = sems
    n = grads_ref.shape[0]
    me = lax.axis_index("dp")
    column = lax.axis_index("tensor")
    barrier = pltpu.get_barrier_semaphore()

    def hello(o, carry):
        pl.semaphore_signal(barrier, inc=1, device_id={"dp": lax.rem(me + o, n)}, device_id_type=MESH)
        return carry

    lax.fori_loop(1, n, hello, 0)
    for o in range(1, 4):
        pl.semaphore_signal(barrier, inc=1, device_id={"tensor": lax.rem(column + o, 4)}, device_id_type=MESH)
    pl.semaphore_wait(barrier, n - 1 + 3)

    def copies(o):
        peer = lax.rem(me + o, n)
        big = pltpu.make_async_remote_copy(
            src_ref=grads_ref.at[peer],
            dst_ref=landed.at[o],
            send_sem=send.at[o],
            recv_sem=recv.at[o],
            device_id={"dp": peer},
            device_id_type=MESH,
        )
        little = pltpu.make_async_remote_copy(
            src_ref=small_ref.at[peer],
            dst_ref=small_landed.at[o],
            send_sem=small_send.at[o],
            recv_sem=small_recv.at[o],
            device_id={"dp": peer},
            device_id_type=MESH,
        )
        return big, little

    def launch_small(o, carry):
        copies(o)[1].start()
        return carry

    def launch(o, carry):
        copies(o)[0].start()
        return carry

    def finish_small(o, total):
        copies(o)[1].wait()
        return total + small_landed[o]

    lax.fori_loop(1, n, launch_small, 0)
    lax.fori_loop(1, n, launch, 0)
    small = lax.fori_loop(1, n, finish_small, small_ref[me])
    small_sum[...] = small
    gain_copies = []
    for o in range(1, 4):
        copy = pltpu.make_async_remote_copy(
            src_ref=small_sum,
            dst_ref=gain_landed.at[o],
            send_sem=gain_send.at[o],
            recv_sem=gain_recv.at[o],
            device_id={"tensor": lax.rem(column + o, 4)},
            device_id_type=MESH,
        )
        copy.start()
        gain_copies.append(copy)
    small_out[0] = small
    for o, copy in enumerate(gain_copies, 1):
        copy.wait()
        small = small + gain_landed[o]
    small_out[1] = small
    out_ref[...] = grads_ref[me].astype(F32)

    def finish(o, carry):
        copies(o)[0].wait()
        out_ref[...] += landed[o].astype(F32)
        return carry

    lax.fori_loop(1, n, finish, 0)


def sum_over_dp(number, grads, small):
    n, rows, width = grads.shape
    dma = pltpu.SemaphoreType.DMA
    return pl.pallas_call(
        sum_kernel,
        out_shape=(whole((rows, width), F32), whole((2,) + small.shape[1:], F32)),
        scratch_shapes=[
            pltpu.VMEM(grads.shape, BF16),
            pltpu.VMEM(small.shape, F32),
            pltpu.VMEM(small.shape[1:], F32),
            pltpu.VMEM((4,) + small.shape[1:], F32),
            dma((n,)),
            dma((n,)),
            dma((n,)),
            dma((n,)),
            dma((4,)),
            dma((4,)),
        ],
        name="sum_over_dp",
        compiler_params=pltpu.CompilerParams(
            collective_id=number, has_side_effects=True, vmem_limit_bytes=60 * 1024 * 1024
        ),
    )(grads, small)


def attend(qkv, base, keep):
    width = qkv.shape[1] // 3
    outs = (
        whole((L, width), BF16),
        whole((width // DH, L, L), BF16),
    )
    if base is None:
        return call(lambda *r: attend_kernel(False, *r), outs, name="cross_fwd")(qkv)
    return call(lambda *r: attend_kernel(True, *r), outs, name="self_fwd")(qkv, base, keep)


def attend_back(qkv, probs, grad_mixed, masked):
    width = qkv.shape[1] // 3
    scratch = (pltpu.VMEM((L, DH), F32), pltpu.VMEM((L, DH), F32))
    grads = whole((L, 3 * width), BF16)
    if masked:
        return call(
            lambda *r: attend_back_kernel(True, *r),
            (grads, whole((width // DH, L), F32)),
            scratch,
            name="self_bwd",
        )(qkv, probs, grad_mixed)
    return call(lambda *r: attend_back_kernel(False, *r), grads, scratch, name="cross_bwd")(
        qkv, probs, grad_mixed
    )


def gather_weights(*parts):
    return lax.all_gather(jnp.concatenate(parts, axis=1), "dp", axis=0, tiled=True)


def scatter_grads(*parts):
    return lax.psum_scatter(to_half(jnp.concatenate(parts, axis=1)), "dp", scatter_dimension=0, tiled=True).astype(F32)


def per_device(
    layer_in,
    encoder_states,
    grad_out,
    buckets,
    keep,
    wq_self,
    wk_self,
    wv_self,
    wo_self,
    wq_cross,
    wk_cross,
    wv_cross,
    wo_cross,
    w_gate,
    w_up,
    w_down,
    norm_scales,
    rel_bias,
):
    W = wq_self.shape[1]
    FFL = w_gate.shape[1]
    D = layer_in.shape[1]
    heads = W // DH
    t_index = lax.axis_index("tensor")
    indicator = jnp.asarray(distance_indicator())
    base_row = jnp.einsum("bm,bh->hm", indicator, rel_bias, precision=lax.Precision.HIGHEST)
    base = jnp.stack([jnp.roll(base_row, s, axis=1) for s in range(8)], axis=1)

    first = gather_weights(
        wq_self, wk_self, wv_self, wo_self.T, wq_cross, wk_cross, wv_cross, wo_cross.T, norm_scales.T
    )
    stream_all = spread(layer_in)
    first, stream_all, others = lax.optimization_barrier(
        (first, stream_all, jnp.concatenate([encoder_states, grad_out], axis=1))
    )
    others = spread(others)
    self_qkv_w = first[:, :3 * W]
    self_out_t = first[:, 3 * W:4 * W]
    cross_q_w = first[:, 4 * W:5 * W]
    cross_kv_w = first[:, 5 * W:7 * W]
    cross_out_t = first[:, 7 * W:8 * W]
    gains = first[:, 8 * W:].T.astype(F32)
    rows_one = to_half(unit_norm(stream_all.astype(F32))[0] * gains[0:1])
    self_qkv = to_half(matmul(rows_one, self_qkv_w))
    mixed_self, probs_self = attend(self_qkv, base, keep[0])
    mixed_self, others, feed_parts = lax.optimization_barrier(
        (mixed_self, others, jnp.concatenate([w_gate, w_up, w_down.T], axis=1))
    )
    second = gather_weights(feed_parts)
    gate_up_w = second[:, :2 * FFL]
    down_t = second[:, 2 * FFL:]
    source_rows = others[:, :D]
    grad_rows = others[:, D:]
    rows_two, stream_one = forward_exchange(1, mixed_self, self_out_t, layer_in, gains[1:2])
    cross_qkv = jnp.concatenate(
        [to_half(matmul(rows_two, cross_q_w)), to_half(matmul(source_rows, cross_kv_w))], axis=1
    )
    mixed_cross, probs_cross = attend(cross_qkv, None, None)
    rows_three, stream_two = forward_exchange(2, mixed_cross, cross_out_t, stream_one, gains[2:3])
    gate_up = matmul(rows_three, gate_up_w)
    up_rows = gate_up[:, FFL:]
    activated, slope = gelu_pair(gate_up[:, :FFL])
    hidden = to_half(activated * up_rows)
    grad_hidden = matmul(grad_rows, down_t)
    grad_gate_up = to_half(
        jnp.concatenate([grad_hidden * up_rows * slope, grad_hidden * activated], axis=1)
    )
    grad_two_rows, grad_stream_two, gain_three = backward_exchange(
        3, True, grad_gate_up, gate_up_w, stream_two, grad_out, gains[2:3]
    )
    grad_third = scatter_grads(
        left_contract(rows_three, grad_gate_up), left_contract(grad_rows, hidden)
    )
    grad_mixed_cross = to_half(matmul(grad_two_rows, cross_out_t))
    grad_cross = attend_back(cross_qkv, probs_cross, grad_mixed_cross, False)
    grad_q_cross = grad_cross[:, :W]
    grad_kv_cross = grad_cross[:, W:]
    grad_one_rows, grad_stream_one, gain_two = backward_exchange(
        4, True, grad_q_cross, cross_q_w, stream_one, grad_stream_two, gains[1:2]
    )
    grad_mixed_self = to_half(matmul(grad_one_rows, self_out_t))
    grad_self, diagonal = attend_back(self_qkv, probs_self, grad_mixed_self, True)
    hidden_late, grad_kv_late, grad_third, _ = lax.optimization_barrier(
        (hidden, grad_kv_cross, grad_third, grad_self)
    )
    late_rows = collect(
        jnp.concatenate(
            [right_contract(hidden_late, down_t), right_contract(grad_kv_late, cross_kv_w)], axis=1
        )
    )
    layer_out = to_half(stream_two + late_rows[:, :D])
    grad_encoder = late_rows[:, D:]
    grad_in, gain_one = backward_exchange(
        5, False, grad_self, self_qkv_w, layer_in, grad_stream_one, gains[0:1]
    )
    bias_part = jnp.einsum("bm,hm->bh", indicator, diagonal, precision=lax.Precision.HIGHEST)
    dp_size = lax.axis_size("dp")
    tensor_size = lax.axis_size("tensor")
    share = D // dp_size
    grads = jnp.concatenate(
        [
            to_half(part)
            for part in (
                left_contract(rows_one, grad_self),
                left_contract(grad_one_rows, mixed_self),
                left_contract(rows_two, grad_q_cross),
                left_contract(source_rows, grad_kv_cross),
                left_contract(grad_two_rows, mixed_cross),
            )
        ],
        axis=1,
    ).reshape(dp_size, share, 8 * W)
    gain_part = jnp.concatenate([gain_one, gain_two, gain_three]).reshape(3, dp_size, share)
    small = jnp.concatenate(
        [
            jnp.pad(gain_part.transpose(1, 0, 2), ((0, 0), (0, 0), (0, 128 - share))),
            jnp.broadcast_to(
                jnp.pad(bias_part.reshape(1, 1, -1), ((0, 0), (0, 0), (0, 128 - NBUCKET * heads))),
                (dp_size, 1, 128),
            ),
            jnp.zeros((dp_size, 4, 128), F32),
        ],
        axis=1,
    )
    summed, small_sums = sum_over_dp(6, grads, small)
    grad_first = summed[:, :4 * W]
    grad_second = summed[:, 4 * W:]
    own = share // tensor_size
    grad_norm_scales = lax.dynamic_slice_in_dim(small_sums[1, :3], t_index * own, own, 1)
    grad_rel_bias = small_sums[0, 3, :NBUCKET * heads].reshape(NBUCKET, heads)
    return (
        layer_out,
        grad_in,
        grad_encoder,
        grad_first[:, :W],
        grad_first[:, W:2 * W],
        grad_first[:, 2 * W:3 * W],
        grad_first[:, 3 * W:].T,
        grad_second[:, :W],
        grad_second[:, W:2 * W],
        grad_second[:, 2 * W:3 * W],
        grad_second[:, 3 * W:].T,
        grad_third[:, :FFL],
        grad_third[:, FFL:2 * FFL],
        grad_third[:, 2 * FFL:].T,
        grad_norm_scales,
        grad_rel_bias,
    )


def solution(mesh):
    in_specs = (
        P(("dp", "tensor"), None),
        P(("dp", "tensor"), None),
        P(("dp", "tensor"), None),
        P("dp", None, None),
        P("dp", None, None),
        P("dp", "tensor"),
        P("dp", "tensor"),
        P("dp", "tensor"),
        P("tensor", "dp"),
        P("dp", "tensor"),
        P("dp", "tensor"),
        P("dp", "tensor"),
        P("tensor", "dp"),
        P("dp", "tensor"),
        P("dp", "tensor"),
        P("tensor", "dp"),
        P(None, "dp"),
        P(None, "tensor"),
    )
    out_specs = (
        P(("dp", "tensor"), None),
        P(("dp", "tensor"), None),
        P(("dp", "tensor"), None),
        P("dp", "tensor"),
        P("dp", "tensor"),
        P("dp", "tensor"),
        P("tensor", "dp"),
        P("dp", "tensor"),
        P("dp", "tensor"),
        P("dp", "tensor"),
        P("tensor", "dp"),
        P("dp", "tensor"),
        P("dp", "tensor"),
        P("tensor", "dp"),
        P(None, ("dp", "tensor")),
        P(None, "tensor"),
    )
    return jax.shard_map(
        per_device, mesh=mesh, in_specs=in_specs, out_specs=out_specs, check_vma=False
    )
```
